32 devices in a mesh: blk: 8 (over y, x, core), rows: 4 (over z).
Axes of the slice: x: 2, y: 2, z: 4, core: 2. Of those that a mesh axis runs over, the one named last changes fastest.
Arguments:
- sens_tiles: bfloat16 [2048, 512, 128], P('blk', 'rows'), may hold values from -1 to 1
- start_basis: bfloat16 [64, 32768], P(None, 'blk'), may hold values from -6 to 6
- row_blocks: int32 [2048, 4], P('blk', 'rows'), may hold values from 0 to 7, as said below
- col_blocks: int32 [2048, 4], P('blk', 'rows'), may hold values from 0 to 31, as said below
- live_counts: int32 [8, 4], P('blk', 'rows'), may hold values from 64 to 256, as said below
Outputs:
- orthonormal: float32 [4, 64, 32768], P(None, None, ('blk', 'rows'))
The draws below stay inside these ranges and needn't reach their ends.
Inputs may be any that keep to these rules, and one draw needn't show every extreme that they name: Within one device the pairs (row_blocks, col_blocks) of its 256 slots are distinct. Within one device the pairs (row_blocks, col_blocks) of its 256 slots are distinct. Slots 0 to live_counts - 1 of a device hold its tiles; some device has all 256 slots live.
All inputs are finite; a program needn't handle non-finite values.
Results may differ from the reference program's by a relative error of at most 0.012.
The reference program's roundings to bfloat16 on the way count: a program that leaves them out, or rounds other values in their place, can miss the bound.
Values may be sent and summed in bfloat16 or wider, within the bound.
A program may use at most 128 MiB of HBM per device.

```python
import math
import jax
import jax.numpy as jnp
from jax import lax

TILE = 128
K = 64
RB = 8
CB = 32
MAXB = 256
ITERS = 4
DATA = 4096
CELLS = 32768
SLOTS = 2048
N_BLK = 8
N_ROWS = 4


grade_span = 3.28


def pattern_pairs(key):
    base = jax.random.fold_in(key, 7)
    keys = jax.random.split(base, N_BLK * N_ROWS)
    orders = jax.vmap(lambda single: jax.random.permutation(single, RB * CB))(keys)[:, :MAXB]
    rows_part = (orders // CB).reshape(N_BLK, N_ROWS, MAXB).transpose(0, 2, 1).reshape(N_BLK * MAXB, N_ROWS)
    cols_part = (orders % CB).reshape(N_BLK, N_ROWS, MAXB).transpose(0, 2, 1).reshape(N_BLK * MAXB, N_ROWS)
    return (rows_part.astype(jnp.int32), cols_part.astype(jnp.int32))


def draw_sens_tiles(key, part):
    rows_part = pattern_pairs(key)[0]
    datum_block = jnp.arange(N_ROWS, dtype=jnp.int32)[None, :] * RB + rows_part
    datum_index = datum_block[:, :, None] * TILE + jnp.arange(TILE, dtype=jnp.int32)[None, None, :]
    ranking = jax.random.permutation(jax.random.fold_in(key, 13), DATA)
    levels = jnp.minimum(ranking, K).astype(jnp.float32) / K
    weights = jnp.exp(-grade_span * levels)
    row_scale = jnp.take(weights, datum_index.reshape(-1)).reshape(SLOTS, N_ROWS * TILE)
    noise_key = jax.random.fold_in(key, 17)
    values = jax.random.truncated_normal(noise_key, -6.0, 6.0, (SLOTS, N_ROWS * TILE, TILE), jnp.float32)
    return (values * (row_scale[:, :, None] / math.sqrt(TILE))).astype(jnp.bfloat16)


def draw_row_blocks(key, part):
    return pattern_pairs(key)[0]


def draw_col_blocks(key, part):
    return pattern_pairs(key)[1]


def draw_live_counts(key, part):
    base = jax.random.fold_in(key, 11)
    first, second = jax.random.split(base)
    divisor = jax.random.randint(first, (N_BLK * N_ROWS,), 1, 5)
    counted = MAXB // divisor
    fullest = jax.random.randint(second, (), 0, N_BLK * N_ROWS)
    counted = jnp.where(jnp.arange(N_BLK * N_ROWS) == fullest, MAXB, counted)
    return counted.reshape(N_BLK, N_ROWS).astype(jnp.int32)


def steps_of(rng, shape, shards, smallest, top_value):
    gain, own = 1.0, jax.random.fold_in(rng, 6)
    for position, parts in shards:
        draws = jnp.exp(jax.random.uniform(jax.random.fold_in(own, position), (parts,), jnp.float32, smallest / len(shards), top_value / len(shards)))
        gain = gain * jnp.repeat(draws, shape[position] // parts).reshape([-1 if axis == position else 1 for axis in range(len(shape))])
    return gain


def scatter_about(own_key, extent, deviation, reach, cuts=(), kind=jnp.bfloat16):
    values = deviation * jax.random.normal(own_key, extent, jnp.float32)
    if cuts:
        values = values * steps_of(own_key, extent, cuts, -0.22, 0.18)
    return jnp.clip(values, -reach, reach).astype(kind)


def setup_inputs(seed: int = 0) -> dict:
    arg_keys = jax.random.split(jax.random.key(seed), 6)
    sens_tiles = draw_sens_tiles(jax.random.fold_in(arg_keys[5], 71), 0)
    start_basis = scatter_about(arg_keys[1], (K, CELLS), 1.0, 6.0, ((1, 8),))
    row_blocks = draw_row_blocks(jax.random.fold_in(arg_keys[5], 71), 0)
    col_blocks = draw_col_blocks(jax.random.fold_in(arg_keys[5], 71), 0)
    live_counts = draw_live_counts(jax.random.fold_in(arg_keys[5], 71), 0)
    return {"sens_tiles": sens_tiles, "start_basis": start_basis, "row_blocks": row_blocks, "col_blocks": col_blocks, "live_counts": live_counts}


def forward_one(tile_set, basis_blocks, row_slots, col_slots, count_live):
    picked = jnp.take(basis_blocks, col_slots, axis=1)
    products = jnp.einsum('kst,sit->ksi', picked, tile_set)
    live = jnp.arange(MAXB) < count_live
    onehot = ((row_slots[None, :] == jnp.arange(RB)[:, None]) & live[None, :]).astype(jnp.float32)
    summed = jnp.einsum('ksi,rs->kri', products, onehot, precision=lax.Precision.HIGHEST)
    return summed.reshape(K, RB * TILE)

def backward_one(tile_set, image_blocks, row_slots, col_slots, count_live):
    picked = jnp.take(image_blocks, row_slots, axis=1)
    products = jnp.einsum('ksi,sij->ksj', picked, tile_set)
    live = jnp.arange(MAXB) < count_live
    onehot = ((col_slots[None, :] == jnp.arange(CB)[:, None]) & live[None, :]).astype(jnp.float32)
    summed = jnp.einsum('ksj,cs->kcj', products, onehot, precision=lax.Precision.HIGHEST)
    return summed.reshape(K, CB * TILE)

def cholesky_qr(current, total):
    gram = jnp.dot(current, current.T, precision=lax.Precision.HIGHEST) / total
    lower = jnp.linalg.cholesky(gram)
    return jax.scipy.linalg.solve_triangular(lower, current, lower=True)

def reference(sens_tiles, start_basis, row_blocks, col_blocks, live_counts):
    tile_grid = sens_tiles.reshape(N_BLK, MAXB, N_ROWS, TILE, TILE)
    row_grid = row_blocks.reshape(N_BLK, MAXB, N_ROWS)
    col_grid = col_blocks.reshape(N_BLK, MAXB, N_ROWS)
    total = float(N_BLK * CB * TILE)
    basis_now = start_basis
    results = []
    for iteration in range(ITERS):
        blocks = basis_now.astype(jnp.float32).reshape(K, N_BLK, CB, TILE)

        def add_block(accum, index):
            tile_set = tile_grid[index].astype(jnp.float32)
            own = blocks[:, index]
            terms = jax.vmap(lambda place: forward_one(tile_set[:, place], own, row_grid[index, :, place], col_grid[index, :, place], live_counts[index, place]))(jnp.arange(N_ROWS))
            return (accum + terms, None)
        image, unused = lax.scan(add_block, jnp.zeros((N_ROWS, K, RB * TILE), jnp.float32), jnp.arange(N_BLK))
        image_half = image.astype(jnp.bfloat16)
        image_float = image_half.astype(jnp.float32).reshape(N_ROWS, K, RB, TILE)

        def back_block(index):
            tile_set = tile_grid[index].astype(jnp.float32)
            terms = jax.vmap(lambda place: backward_one(tile_set[:, place], image_float[place], row_grid[index, :, place], col_grid[index, :, place], live_counts[index, place]))(jnp.arange(N_ROWS))
            return jnp.sum(terms, axis=0)
        hessian = lax.map(back_block, jnp.arange(N_BLK))
        hessian = jnp.transpose(hessian, (1, 0, 2)).reshape(K, N_BLK * CB * TILE)
        result = cholesky_qr(hessian, total)
        results.append(result)
        basis_now = result.astype(jnp.bfloat16)
    return jnp.stack(results, axis=0)
```

```python
import functools

import jax
import jax.numpy as jnp
from jax import lax
from jax.experimental import pallas as pl
from jax.experimental.pallas import tpu as pltpu
from jax.sharding import PartitionSpec as P

RB = 8
CB = 32
ITERS = 4
MESH = pl.DeviceIdType.MESH
F32 = jnp.float32
BF16 = jnp.bfloat16
HIGHEST = lax.Precision.HIGHEST


def aligned(index, width):
    return pl.ds(pl.multiple_of(index * width, width), width)


def inverse_factor(gram):
    size = gram.shape[0]
    row_id = lax.broadcasted_iota(jnp.int32, (size, size), 0)
    lane_id = lax.broadcasted_iota(jnp.int32, (size, size), 1)
    eye = (row_id == lane_id).astype(F32)
    whole = jnp.concatenate([gram, eye], axis=1)
    step = 8
    blocks = [whole[b * step : (b + 1) * step, :] for b in range(size // step)]
    sub_id = lax.broadcasted_iota(jnp.int32, (step, 2 * size), 0)
    for j in range(size):
        home, within = divmod(j, step)
        row = blocks[home][within : within + 1, :]
        scaled = row / row[:, j : j + 1]
        for b in range(home, size // step):
            update = blocks[b][:, j : j + 1] * scaled
            if b == home:
                update = jnp.where(sub_id > within, update, 0.0)
            blocks[b] = blocks[b] - update
    whole = jnp.concatenate(blocks, axis=0)
    pivots = jnp.sum(whole[:, :size] * eye, axis=1, keepdims=True)
    return whole[:, size:] * (1.0 / jnp.sqrt(pivots))


def kernel(
    n,
    m,
    total,
    inv_ref,
    tiles_hbm,
    start_ref,
    out_ref,
    tiles,
    dense,
    basis,
    part,
    rs_buf,
    half_own,
    half,
    hess_own,
    up_out,
    up_buf,
    down_out,
    down_buf,
    gram_own,
    gram_rows,
    gram_line,
    gram_blk,
    load_sem,
    rs_send,
    rs_recv,
    ag_send,
    ag_recv,
    up_send,
    up_recv,
    down_send,
    down_recv,
    gr_send,
    gr_recv,
    gb_send,
    gb_recv,
    bu_send,
    bu_recv,
    bd_send,
    bd_recv,
):
    slots = tiles_hbm.shape[0]
    tile = tiles_hbm.shape[1]
    vectors = start_ref.shape[0]
    data = RB * tile
    cells = start_ref.shape[1]
    width = cells // m
    owners = min(n, RB)
    span = data // owners
    b = lax.axis_index("blk")
    z = lax.axis_index("rows")

    load = pltpu.make_async_copy(tiles_hbm, tiles.at[pl.ds(0, slots)], load_sem)
    load.start()

    barrier = pltpu.get_barrier_semaphore()

    @pl.loop(1, n)
    def _(d):
        pl.semaphore_signal(
            barrier, inc=1, device_id={"blk": lax.rem(b + d, n)}, device_id_type=MESH
        )

    @pl.loop(1, m)
    def _(d):
        pl.semaphore_signal(
            barrier, inc=1, device_id={"rows": lax.rem(z + d, m)}, device_id_type=MESH
        )

    tiles[slots] = jnp.zeros((tile, tile), BF16)
    basis[...] = start_ref[...]
    load.wait()

    @pl.loop(0, RB)
    def _(r):
        @pl.loop(0, CB)
        def _(c):
            dense[aligned(r, tile), aligned(c, tile)] = tiles[inv_ref[r * CB + c]]

    pl.semaphore_wait(barrier, n - 1 + m - 1)

    def copy(src, dst, send_sem, recv_sem, where):
        return pltpu.make_async_remote_copy(
            src_ref=src,
            dst_ref=dst,
            send_sem=send_sem,
            recv_sem=recv_sem,
            device_id=where,
            device_id_type=MESH,
        )

    def rs_copy(dest, slot):
        return copy(
            part.at[:, aligned(dest, span)],
            rs_buf.at[slot],
            rs_send.at[dest],
            rs_recv.at[slot],
            {"blk": dest},
        )

    def ag_copy(dest, chunk):
        return copy(
            half_own,
            half.at[:, aligned(chunk, span)],
            ag_send.at[dest],
            ag_recv.at[chunk],
            {"blk": dest},
        )

    def up_copy(c):
        return copy(up_out.at[c], up_buf.at[c], up_send.at[c], up_recv.at[c], {"rows": z + 1})

    def down_copy(c):
        return copy(
            down_out.at[c], down_buf.at[c], down_send.at[c], down_recv.at[c], {"rows": z - 1}
        )

    def gr_copy(dest, slot):
        return copy(
            gram_own, gram_rows.at[slot], gr_send.at[dest], gr_recv.at[slot], {"rows": dest}
        )

    def gb_copy(dest, slot):
        return copy(
            gram_line, gram_blk.at[slot], gb_send.at[dest], gb_recv.at[slot], {"blk": dest}
        )

    def bu_copy(c):
        chunk = basis.at[:, aligned(c, width)]
        return copy(chunk, chunk, bu_send.at[c], bu_recv.at[c], {"rows": z + 1})

    def bd_copy(c):
        chunk = basis.at[:, aligned(c, width)]
        return copy(chunk, chunk, bd_send.at[c], bd_recv.at[c], {"rows": z - 1})

    def forward(c):
        return lax.dot_general(
            basis[:, aligned(c, width)],
            dense[:, aligned(c, width)],
            (((1,), (1,)), ((), ())),
            preferred_element_type=F32,
        )

    def backward(c):
        return jnp.dot(half[...], dense[:, aligned(c, width)], preferred_element_type=F32)

    @pl.loop(0, ITERS)
    def _(it):
        part[...] = forward(z)
        for d in range(1, m):

            @pl.when(z - d >= 0)
            def _():
                c = z - d

                @pl.when(it > 0)
                def _():
                    bu_copy(c).wait_recv()

                    @pl.when(z + 1 < m)
                    def _():
                        bu_copy(c).start()

                part[...] += forward(c)

            @pl.when(z + d < m)
            def _():
                c = z + d

                @pl.when(it > 0)
                def _():
                    bd_copy(c).wait_recv()

                    @pl.when(z > 0)
                    def _():
                        bd_copy(c).start()

                part[...] += forward(c)

        @pl.loop(0, owners)
        def _(q):
            @pl.when(q != b)
            def _():
                rs_copy(q, b).start()

        @pl.when(b < owners)
        def _():
            own = part[:, aligned(b, span)]

            def add(d, acc):
                src = lax.rem(b + d, n)
                rs_copy(b, src).wait_recv()
                return acc + rs_buf[src]

            own = lax.fori_loop(1, n, add, own)
            half_own[...] = own.astype(BF16)

            @pl.loop(1, n)
            def _(d):
                ag_copy(lax.rem(b + d, n), b).start()

            half[:, aligned(b, span)] = half_own[...]

        @pl.loop(0, owners)
        def _(q):
            @pl.when(q != b)
            def _():
                ag_copy(b, q).wait_recv()
                rs_copy(q, b).wait_send()

        for k in range(m - 1):
            c = m - 1 - k

            @pl.when(c > z)
            def _():
                mine = backward(c)

                @pl.when(z > 0)
                def _():
                    up_copy(c).wait_recv()
                    up_out[c] = mine + up_buf[c]

                @pl.when(z == 0)
                def _():
                    up_out[c] = mine

                up_copy(c).start()

            e = k

            @pl.when(e < z)
            def _():
                mine = backward(e)

                @pl.when(z < m - 1)
                def _():
                    down_copy(e).wait_recv()
                    down_out[e] = mine + down_buf[e]

                @pl.when(z == m - 1)
                def _():
                    down_out[e] = mine

                down_copy(e).start()

        hess_own[...] = backward(z)

        @pl.when(z > 0)
        def _():
            up_copy(z).wait_recv()
            hess_own[...] += up_buf[z]

        @pl.when(z < m - 1)
        def _():
            down_copy(z).wait_recv()
            hess_own[...] += down_buf[z]

        @pl.when(it > 0)
        def _():
            for c in range(m):

                @pl.when(jnp.logical_and(c <= z, z + 1 < m))
                def _():
                    bu_copy(c).wait_send()

                @pl.when(jnp.logical_and(c >= z, z > 0))
                def _():
                    bd_copy(c).wait_send()

        hess = hess_own[...]
        gram = lax.dot_general(
            hess, hess, (((1,), (1,)), ((), ())), precision=HIGHEST, preferred_element_type=F32
        )
        fold = vectors // 2
        gram_own[...] = jnp.concatenate([gram[:fold], gram[fold:]], axis=1)

        @pl.loop(1, m)
        def _(d):
            gr_copy(lax.rem(z + d, m), z).start()

        def add_line(d, acc):
            src = lax.rem(z + d, m)
            gr_copy(z, src).wait_recv()
            return acc + gram_rows[src]

        gram_line[...] = lax.fori_loop(1, m, add_line, gram_own[...])

        @pl.loop(1, n)
        def _(d):
            gb_copy(lax.rem(b + d, n), b).start()

        def add_blk(d, acc):
            src = lax.rem(b + d, n)
            gb_copy(b, src).wait_recv()
            return acc + gram_blk[src]

        packed = lax.fori_loop(1, n, add_blk, gram_line[...])
        gram = jnp.concatenate([packed[:, :vectors], packed[:, vectors:]], axis=0) / total

        for c in range(m):

            @pl.when(c > z)
            def _():
                up_copy(c).wait_send()

            @pl.when(c < z)
            def _():
                down_copy(c).wait_send()

        @pl.loop(1, m)
        def _(d):
            gr_copy(lax.rem(z + d, m), z).wait_send()

        @pl.loop(1, n)
        def _(d):
            gb_copy(lax.rem(b + d, n), b).wait_send()

        @pl.when(b < owners)
        def _():
            @pl.loop(1, n)
            def _(d):
                ag_copy(lax.rem(b + d, n), b).wait_send()

        result = jnp.dot(
            inverse_factor(gram), hess_own[...], precision=HIGHEST, preferred_element_type=F32
        )
        basis[:, aligned(z, width)] = result.astype(BF16)

        @pl.when(it < ITERS - 1)
        def _():
            @pl.when(z + 1 < m)
            def _():
                bu_copy(z).start()

            @pl.when(z > 0)
            def _():
                bd_copy(z).start()

        out_ref[it] = result


def local(n, m, sens_tiles, start_basis, row_blocks, col_blocks, live_counts):
    slots, tile = sens_tiles.shape[0], sens_tiles.shape[2]
    vectors, cells = start_basis.shape
    data, width = RB * tile, cells // m
    span = data // min(n, RB)
    numbers = jnp.arange(slots, dtype=jnp.int32)
    places = row_blocks[:, 0] * CB + col_blocks[:, 0]
    hit = (places[None, :] == jnp.arange(RB * CB, dtype=jnp.int32)[:, None]) & (
        numbers < live_counts[0, 0]
    )[None, :]
    inv = jnp.min(jnp.where(hit, numbers[None, :], slots), axis=1)
    total = float(cells * n)
    dma = pltpu.SemaphoreType.DMA
    return pl.pallas_call(
        functools.partial(kernel, n, m, total),
        out_shape=jax.ShapeDtypeStruct((ITERS, vectors, width), F32),
        in_specs=[
            pl.BlockSpec(memory_space=pltpu.SMEM),
            pl.BlockSpec(memory_space=pl.ANY),
            pl.BlockSpec(memory_space=pltpu.VMEM),
        ],
        out_specs=pl.BlockSpec(memory_space=pltpu.VMEM),
        scratch_shapes=[
            pltpu.VMEM((slots + 1, tile, tile), BF16),
            pltpu.VMEM((data, cells), BF16),
            pltpu.VMEM((vectors, cells), BF16),
            pltpu.VMEM((vectors, data), F32),
            pltpu.VMEM((n, vectors, span), F32),
            pltpu.VMEM((vectors, span), BF16),
            pltpu.VMEM((vectors, data), BF16),
            pltpu.VMEM((vectors, width), F32),
            pltpu.VMEM((m, vectors, width), F32),
            pltpu.VMEM((m, vectors, width), F32),
            pltpu.VMEM((m, vectors, width), F32),
            pltpu.VMEM((m, vectors, width), F32),
            pltpu.VMEM((vectors // 2, vectors * 2), F32),
            pltpu.VMEM((m, vectors // 2, vectors * 2), F32),
            pltpu.VMEM((vectors // 2, vectors * 2), F32),
            pltpu.VMEM((n, vectors // 2, vectors * 2), F32),
            dma,
            dma((n,)),
            dma((n,)),
            dma((n,)),
            dma((n,)),
            dma((m,)),
            dma((m,)),
            dma((m,)),
            dma((m,)),
            dma((m,)),
            dma((m,)),
            dma((n,)),
            dma((n,)),
            dma((m,)),
            dma((m,)),
            dma((m,)),
            dma((m,)),
        ],
        compiler_params=pltpu.CompilerParams(
            collective_id=0, has_side_effects=True, vmem_limit_bytes=56 * 1024 * 1024
        ),
        name="subspace",
    )(inv, sens_tiles, start_basis)


def solution(mesh):
    in_specs = (
        P("blk", "rows", None),
        P(None, "blk"),
        P("blk", "rows"),
        P("blk", "rows"),
        P("blk", "rows"),
    )
    out_specs = P(None, None, ("blk", "rows"))
    return jax.shard_map(
        functools.partial(local, mesh.shape["blk"], mesh.shape["rows"]),
        mesh=mesh,
        in_specs=in_specs,
        out_specs=out_specs,
        check_vma=False,
    )
```

```python
import functools

import jax
import jax.numpy as jnp
from jax import lax
from jax.experimental import pallas as pl
from jax.experimental.pallas import tpu as pltpu
from jax.sharding import PartitionSpec as P

RB = 8
CB = 32
ITERS = 4
MESH = pl.DeviceIdType.MESH
F32 = jnp.float32
BF16 = jnp.bfloat16
HIGHEST = lax.Precision.HIGHEST
CODE = jnp.int16
TOP = 32767.0
PIECES = 2


def aligned(index, width):
    return pl.ds(pl.multiple_of(index * width, width), width)


def inverse_factor(gram):
    size = gram.shape[0]
    row_id = lax.broadcasted_iota(jnp.int32, (size, size), 0)
    lane_id = lax.broadcasted_iota(jnp.int32, (size, size), 1)
    eye = (row_id == lane_id).astype(F32)
    whole = jnp.concatenate([gram, eye], axis=1)
    step = 8
    blocks = [whole[b * step : (b + 1) * step, :] for b in range(size // step)]
    sub_id = lax.broadcasted_iota(jnp.int32, (step, 2 * size), 0)
    for j in range(size):
        home, within = divmod(j, step)
        row = blocks[home][within : within + 1, :]
        scaled = row / row[:, j : j + 1]
        for b in range(home, size // step):
            update = blocks[b][:, j : j + 1] * scaled
            if b == home:
                update = jnp.where(sub_id > within, update, 0.0)
            blocks[b] = blocks[b] - update
    whole = jnp.concatenate(blocks, axis=0)
    pivots = jnp.sum(whole[:, :size] * eye, axis=1, keepdims=True)
    return whole[:, size:] * (1.0 / jnp.sqrt(pivots))


def diagonal_of(size):
    row_id = lax.broadcasted_iota(jnp.int32, (size, size), 0)
    return row_id == lax.broadcasted_iota(jnp.int32, (size, size), 1)


def encode(values, code_ref, scale_ref):
    size = values.shape[0]
    top = jnp.maximum(jnp.max(jnp.abs(values), axis=1, keepdims=True), 1e-30)
    code_ref[...] = jnp.round(values * (TOP / top)).astype(jnp.int32).astype(CODE)
    along = jnp.sum(jnp.where(diagonal_of(size), top * (1.0 / TOP), 0.0), axis=0, keepdims=True)
    scale_ref[:, :size] = jnp.broadcast_to(along, (8, size))
    scale_ref[:, size:] = jnp.broadcast_to(along, (8, size))


def decode(code_ref, scale_ref):
    size = code_ref.shape[0]
    along = scale_ref[0:1, :size]
    scale = jnp.sum(jnp.where(diagonal_of(size), along, 0.0), axis=1, keepdims=True)
    return code_ref[...].astype(F32) * scale


def kernel(
    n,
    m,
    total,
    inv_ref,
    tiles_hbm,
    start_ref,
    out_ref,
    tiles,
    dense,
    basis,
    part,
    rs_buf,
    half_own,
    half,
    hess_own,
    up_out,
    up_buf,
    down_out,
    down_buf,
    up_out_scale,
    up_scale,
    down_out_scale,
    down_scale,
    up_sum,
    down_sum,
    gram_own,
    gram_rows,
    gram_line,
    gram_blk,
    load_sem,
    rs_send,
    rs_recv,
    ag_send,
    ag_recv,
    up_send,
    up_recv,
    down_send,
    down_recv,
    gr_send,
    gr_recv,
    gb_send,
    gb_recv,
    bu_send,
    bu_recv,
    bd_send,
    bd_recv,
    us_send,
    us_recv,
    ds_send,
    ds_recv,
):
    slots = tiles_hbm.shape[0]
    tile = tiles_hbm.shape[1]
    vectors = start_ref.shape[0]
    data = RB * tile
    cells = start_ref.shape[1]
    width = cells // m
    owners = min(n, RB)
    span = data // owners
    b = lax.axis_index("blk")
    z = lax.axis_index("rows")

    load = pltpu.make_async_copy(tiles_hbm, tiles.at[pl.ds(0, slots)], load_sem)
    load.start()

    barrier = pltpu.get_barrier_semaphore()

    @pl.loop(1, n)
    def _(d):
        pl.semaphore_signal(
            barrier, inc=1, device_id={"blk": lax.rem(b + d, n)}, device_id_type=MESH
        )

    @pl.loop(1, m)
    def _(d):
        pl.semaphore_signal(
            barrier, inc=1, device_id={"rows": lax.rem(z + d, m)}, device_id_type=MESH
        )

    tiles[slots] = jnp.zeros((tile, tile), BF16)
    basis[...] = start_ref[...]
    load.wait()

    @pl.loop(0, RB)
    def _(r):
        @pl.loop(0, CB)
        def _(c):
            dense[aligned(r, tile), aligned(c, tile)] = tiles[inv_ref[r * CB + c]]

    pl.semaphore_wait(barrier, n - 1 + m - 1)

    def copy(src, dst, send_sem, recv_sem, where):
        return pltpu.make_async_remote_copy(
            src_ref=src,
            dst_ref=dst,
            send_sem=send_sem,
            recv_sem=recv_sem,
            device_id=where,
            device_id_type=MESH,
        )

    def rs_copy(dest, slot):
        return copy(
            part.at[:, aligned(dest, span)],
            rs_buf.at[slot],
            rs_send.at[dest],
            rs_recv.at[slot],
            {"blk": dest},
        )

    def ag_copy(dest, chunk):
        return copy(
            half_own,
            half.at[:, aligned(chunk, span)],
            ag_send.at[dest],
            ag_recv.at[chunk],
            {"blk": dest},
        )

    def up_copies(c):
        there = {"rows": z + 1}
        return (
            copy(up_out_scale.at[c], up_scale.at[c], us_send.at[c], us_recv.at[c], there),
            copy(up_out.at[c], up_buf.at[c], up_send.at[c], up_recv.at[c], there),
        )

    def down_copies(c):
        there = {"rows": z - 1}
        return (
            copy(down_out_scale.at[c], down_scale.at[c], ds_send.at[c], ds_recv.at[c], there),
            copy(down_out.at[c], down_buf.at[c], down_send.at[c], down_recv.at[c], there),
        )

    def start(copies):
        for each in copies:
            each.start()

    def wait_recv(copies):
        for each in copies:
            each.wait_recv()

    def wait_send(copies):
        for each in copies:
            each.wait_send()

    def gr_copy(dest, slot):
        return copy(
            gram_own, gram_rows.at[slot], gr_send.at[dest], gr_recv.at[slot], {"rows": dest}
        )

    def gb_copy(dest, slot):
        return copy(
            gram_line, gram_blk.at[slot], gb_send.at[dest], gb_recv.at[slot], {"blk": dest}
        )

    piece = width // PIECES

    def bu_copy(c, p):
        k = c * PIECES + p
        chunk = basis.at[:, aligned(k, piece)]
        return copy(chunk, chunk, bu_send.at[k], bu_recv.at[k], {"rows": z + 1})

    def bd_copy(c, p):
        k = c * PIECES + p
        chunk = basis.at[:, aligned(k, piece)]
        return copy(chunk, chunk, bd_send.at[k], bd_recv.at[k], {"rows": z - 1})

    def forward(c):
        return lax.dot_general(
            basis[:, aligned(c, width)],
            dense[:, aligned(c, width)],
            (((1,), (1,)), ((), ())),
            preferred_element_type=F32,
        )

    def backward(c):
        return jnp.dot(half[...], dense[:, aligned(c, width)], preferred_element_type=F32)

    @pl.loop(0, ITERS)
    def _(it):
        part[...] = forward(z)
        for d in range(1, m):
            for p in range(PIECES):

                @pl.when(jnp.logical_and(it > 0, z - d >= 0))
                def _():
                    bu_copy(z - d, p).wait_recv()

                    @pl.when(z + 1 < m)
                    def _():
                        bu_copy(z - d, p).start()

                @pl.when(jnp.logical_and(it > 0, z + d < m))
                def _():
                    bd_copy(z + d, p).wait_recv()

                    @pl.when(z > 0)
                    def _():
                        bd_copy(z + d, p).start()

            @pl.when(z - d >= 0)
            def _():
                part[...] += forward(z - d)

            @pl.when(z + d < m)
            def _():
                part[...] += forward(z + d)

        @pl.loop(0, owners)
        def _(q):
            @pl.when(q != b)
            def _():
                rs_copy(q, b).start()

        @pl.when(b < owners)
        def _():
            own = part[:, aligned(b, span)]

            def add(d, acc):
                src = lax.rem(b + d, n)
                rs_copy(b, src).wait_recv()
                return acc + rs_buf[src]

            own = lax.fori_loop(1, n, add, own)
            half_own[...] = own.astype(BF16)

            @pl.loop(1, n)
            def _(d):
                ag_copy(lax.rem(b + d, n), b).start()

            half[:, aligned(b, span)] = half_own[...]

        @pl.loop(0, owners)
        def _(q):
            @pl.when(q != b)
            def _():
                ag_copy(b, q).wait_recv()
                rs_copy(q, b).wait_send()

        for k in range(m - 1):
            c = m - 1 - k

            @pl.when(c > z)
            def _():
                up_sum[...] = backward(c)

                @pl.when(z > 0)
                def _():
                    wait_recv(up_copies(c))
                    up_sum[...] += decode(up_buf.at[c], up_scale.at[c])

                encode(up_sum[...], up_out.at[c], up_out_scale.at[c])
                start(up_copies(c))

            e = k

            @pl.when(e < z)
            def _():
                down_sum[...] = backward(e)

                @pl.when(z < m - 1)
                def _():
                    wait_recv(down_copies(e))
                    down_sum[...] += decode(down_buf.at[e], down_scale.at[e])

                encode(down_sum[...], down_out.at[e], down_out_scale.at[e])
                start(down_copies(e))

        hess_own[...] = backward(z)

        @pl.when(z > 0)
        def _():
            wait_recv(up_copies(z))
            hess_own[...] += decode(up_buf.at[z], up_scale.at[z])

        @pl.when(z < m - 1)
        def _():
            wait_recv(down_copies(z))
            hess_own[...] += decode(down_buf.at[z], down_scale.at[z])

        @pl.when(it > 0)
        def _():
            for c in range(m):
                for p in range(PIECES):

                    @pl.when(jnp.logical_and(c <= z, z + 1 < m))
                    def _():
                        bu_copy(c, p).wait_send()

                    @pl.when(jnp.logical_and(c >= z, z > 0))
                    def _():
                        bd_copy(c, p).wait_send()

        hess = hess_own[...]
        gram = lax.dot_general(
            hess, hess, (((1,), (1,)), ((), ())), precision=HIGHEST, preferred_element_type=F32
        )
        fold = vectors // 2
        gram_own[...] = jnp.concatenate([gram[:fold], gram[fold:]], axis=1)

        @pl.loop(1, m)
        def _(d):
            gr_copy(lax.rem(z + d, m), z).start()

        def add_line(d, acc):
            src = lax.rem(z + d, m)
            gr_copy(z, src).wait_recv()
            return acc + gram_rows[src]

        gram_line[...] = lax.fori_loop(1, m, add_line, gram_own[...])

        @pl.loop(1, n)
        def _(d):
            gb_copy(lax.rem(b + d, n), b).start()

        def add_blk(d, acc):
            src = lax.rem(b + d, n)
            gb_copy(b, src).wait_recv()
            return acc + gram_blk[src]

        packed = lax.fori_loop(1, n, add_blk, gram_line[...])
        gram = jnp.concatenate([packed[:, :vectors], packed[:, vectors:]], axis=0) / total

        for c in range(m):

            @pl.when(c > z)
            def _():
                wait_send(up_copies(c))

            @pl.when(c < z)
            def _():
                wait_send(down_copies(c))

        @pl.loop(1, m)
        def _(d):
            gr_copy(lax.rem(z + d, m), z).wait_send()

        @pl.loop(1, n)
        def _(d):
            gb_copy(lax.rem(b + d, n), b).wait_send()

        @pl.when(b < owners)
        def _():
            @pl.loop(1, n)
            def _(d):
                ag_copy(lax.rem(b + d, n), b).wait_send()

        result = jnp.dot(
            inverse_factor(gram), hess_own[...], precision=HIGHEST, preferred_element_type=F32
        )
        basis[:, aligned(z, width)] = result.astype(BF16)

        @pl.when(it < ITERS - 1)
        def _():
            for p in range(PIECES):

                @pl.when(z + 1 < m)
                def _():
                    bu_copy(z, p).start()

                @pl.when(z > 0)
                def _():
                    bd_copy(z, p).start()

        out_ref[it] = result


def local(n, m, sens_tiles, start_basis, row_blocks, col_blocks, live_counts):
    slots, tile = sens_tiles.shape[0], sens_tiles.shape[2]
    vectors, cells = start_basis.shape
    data, width = RB * tile, cells // m
    span = data // min(n, RB)
    numbers = jnp.arange(slots, dtype=jnp.int32)
    places = row_blocks[:, 0] * CB + col_blocks[:, 0]
    hit = (places[None, :] == jnp.arange(RB * CB, dtype=jnp.int32)[:, None]) & (
        numbers < live_counts[0, 0]
    )[None, :]
    inv = jnp.min(jnp.where(hit, numbers[None, :], slots), axis=1)
    total = float(cells * n)
    dma = pltpu.SemaphoreType.DMA
    return pl.pallas_call(
        functools.partial(kernel, n, m, total),
        out_shape=jax.ShapeDtypeStruct((ITERS, vectors, width), F32),
        in_specs=[
            pl.BlockSpec(memory_space=pltpu.SMEM),
            pl.BlockSpec(memory_space=pl.ANY),
            pl.BlockSpec(memory_space=pltpu.VMEM),
        ],
        out_specs=pl.BlockSpec(memory_space=pltpu.VMEM),
        scratch_shapes=[
            pltpu.VMEM((slots + 1, tile, tile), BF16),
            pltpu.VMEM((data, cells), BF16),
            pltpu.VMEM((vectors, cells), BF16),
            pltpu.VMEM((vectors, data), F32),
            pltpu.VMEM((n, vectors, span), F32),
            pltpu.VMEM((vectors, span), BF16),
            pltpu.VMEM((vectors, data), BF16),
            pltpu.VMEM((vectors, width), F32),
            pltpu.VMEM((m, vectors, width), CODE),
            pltpu.VMEM((m, vectors, width), CODE),
            pltpu.VMEM((m, vectors, width), CODE),
            pltpu.VMEM((m, vectors, width), CODE),
            pltpu.VMEM((m, 8, vectors * 2), F32),
            pltpu.VMEM((m, 8, vectors * 2), F32),
            pltpu.VMEM((m, 8, vectors * 2), F32),
            pltpu.VMEM((m, 8, vectors * 2), F32),
            pltpu.VMEM((vectors, width), F32),
            pltpu.VMEM((vectors, width), F32),
            pltpu.VMEM((vectors // 2, vectors * 2), F32),
            pltpu.VMEM((m, vectors // 2, vectors * 2), F32),
            pltpu.VMEM((vectors // 2, vectors * 2), F32),
            pltpu.VMEM((n, vectors // 2, vectors * 2), F32),
            dma,
            dma((n,)),
            dma((n,)),
            dma((n,)),
            dma((n,)),
            dma((m,)),
            dma((m,)),
            dma((m,)),
            dma((m,)),
            dma((m,)),
            dma((m,)),
            dma((n,)),
            dma((n,)),
            dma((m * PIECES,)),
            dma((m * PIECES,)),
            dma((m * PIECES,)),
            dma((m * PIECES,)),
            dma((m,)),
            dma((m,)),
            dma((m,)),
            dma((m,)),
        ],
        compiler_params=pltpu.CompilerParams(
            collective_id=0, has_side_effects=True, vmem_limit_bytes=56 * 1024 * 1024
        ),
        name="subspace",
    )(inv, sens_tiles, start_basis)


def solution(mesh):
    in_specs = (
        P("blk", "rows", None),
        P(None, "blk"),
        P("blk", "rows"),
        P("blk", "rows"),
        P("blk", "rows"),
    )
    out_specs = P(None, None, ("blk", "rows"))
    return jax.shard_map(
        functools.partial(local, mesh.shape["blk"], mesh.shape["rows"]),
        mesh=mesh,
        in_specs=in_specs,
        out_specs=out_specs,
        check_vma=False,
    )
```

```python
import functools

import jax
import jax.numpy as jnp
from jax import lax
from jax.experimental import pallas as pl
from jax.experimental.pallas import tpu as pltpu
from jax.sharding import PartitionSpec as P

RB = 8
CB = 32
ITERS = 4
MESH = pl.DeviceIdType.MESH
F32 = jnp.float32
BF16 = jnp.bfloat16
HIGHEST = lax.Precision.HIGHEST
CODE = jnp.int16
TOP = 32767.0
PIECES = 2
SPLIT = 2


def aligned(index, width):
    return pl.ds(pl.multiple_of(index * width, width), width)


def inverse_factor(gram):
    size = gram.shape[0]
    row_id = lax.broadcasted_iota(jnp.int32, (size, size), 0)
    lane_id = lax.broadcasted_iota(jnp.int32, (size, size), 1)
    eye = (row_id == lane_id).astype(F32)
    whole = jnp.concatenate([gram, eye], axis=1)
    step, group = 8, 4
    lanes = 2 * size
    blocks = [whole[k * step : (k + 1) * step, :] for k in range(size // step)]
    sub_id = lax.broadcasted_iota(jnp.int32, (step, lanes), 0)
    for first in range(0, size, group):
        home, within = divmod(first, step)
        rows = [blocks[home][within + g : within + g + 1, :] for g in range(group)]
        entry = [
            [jnp.broadcast_to(row[:, first + g : first + g + 1], (1, lanes)) for g in range(group)]
            for row in rows
        ]
        columns = {
            k: [
                jnp.broadcast_to(blocks[k][:, first + g : first + g + 1], (step, lanes))
                for g in range(group)
            ]
            for k in range(home, size // step)
        }
        for g in range(group):
            over = 1.0 / entry[g][g]
            scaled = rows[g] * over
            ratio = [entry[g][h] * over for h in range(group)]
            for k in range(home, size // step):
                column = columns[k][g]
                if k == home:
                    column = jnp.where(sub_id > within + g, column, 0.0)
                blocks[k] = blocks[k] - column * scaled
                for h in range(g + 1, group):
                    columns[k][h] = columns[k][h] - column * ratio[h]
            for low in range(g + 1, group):
                factor = entry[low][g]
                rows[low] = rows[low] - factor * scaled
                for h in range(g + 1, group):
                    entry[low][h] = entry[low][h] - factor * ratio[h]
    whole = jnp.concatenate(blocks, axis=0)
    pivots = jnp.sum(whole[:, :size] * eye, axis=1, keepdims=True)
    return whole[:, size:] * (1.0 / jnp.sqrt(pivots))


def diagonal_of(size):
    row_id = lax.broadcasted_iota(jnp.int32, (size, size), 0)
    return row_id == lax.broadcasted_iota(jnp.int32, (size, size), 1)


def encode(values, code_ref, scale_ref):
    size = values.shape[0]
    top = jnp.maximum(jnp.max(jnp.abs(values), axis=1, keepdims=True), 1e-30)
    code_ref[...] = jnp.round(values * (TOP / top)).astype(jnp.int32).astype(CODE)
    along = jnp.sum(jnp.where(diagonal_of(size), top * (1.0 / TOP), 0.0), axis=0, keepdims=True)
    scale_ref[:, :size] = jnp.broadcast_to(along, (8, size))
    scale_ref[:, size:] = jnp.broadcast_to(along, (8, size))


def decode(code_ref, scale_ref):
    size = code_ref.shape[0]
    along = scale_ref[0:1, :size]
    scale = jnp.sum(jnp.where(diagonal_of(size), along, 0.0), axis=1, keepdims=True)
    return code_ref[...].astype(F32) * scale


def kernel(
    n,
    m,
    total,
    inv_ref,
    tiles_hbm,
    start_ref,
    out_ref,
    tiles,
    dense,
    basis,
    part,
    rs_buf,
    half_own,
    half,
    hess_own,
    up_out,
    up_buf,
    down_out,
    down_buf,
    up_out_scale,
    up_scale,
    down_out_scale,
    down_scale,
    up_sum,
    down_sum,
    gram_own,
    gram_rows,
    gram_line,
    gram_blk,
    load_sem,
    rs_send,
    rs_recv,
    ag_send,
    ag_recv,
    up_send,
    up_recv,
    down_send,
    down_recv,
    gr_send,
    gr_recv,
    gb_send,
    gb_recv,
    bu_send,
    bu_recv,
    bd_send,
    bd_recv,
    us_send,
    us_recv,
    ds_send,
    ds_recv,
):
    slots = tiles_hbm.shape[0]
    tile = tiles_hbm.shape[1]
    vectors = start_ref.shape[0]
    data = RB * tile
    cells = start_ref.shape[1]
    width = cells // m
    owners = min(n, RB)
    span = data // owners
    b = lax.axis_index("blk")
    z = lax.axis_index("rows")

    load = pltpu.make_async_copy(tiles_hbm, tiles.at[pl.ds(0, slots)], load_sem)
    load.start()

    barrier = pltpu.get_barrier_semaphore()

    @pl.loop(1, n)
    def _(d):
        pl.semaphore_signal(
            barrier, inc=1, device_id={"blk": lax.rem(b + d, n)}, device_id_type=MESH
        )

    @pl.loop(1, m)
    def _(d):
        pl.semaphore_signal(
            barrier, inc=1, device_id={"rows": lax.rem(z + d, m)}, device_id_type=MESH
        )

    tiles[slots] = jnp.zeros((tile, tile), BF16)
    basis[...] = start_ref[...]
    load.wait()

    @pl.loop(0, RB)
    def _(r):
        @pl.loop(0, CB)
        def _(c):
            dense[aligned(r, tile), aligned(c, tile)] = tiles[inv_ref[r * CB + c]]

    pl.semaphore_wait(barrier, n - 1 + m - 1)

    def copy(src, dst, send_sem, recv_sem, where):
        return pltpu.make_async_remote_copy(
            src_ref=src,
            dst_ref=dst,
            send_sem=send_sem,
            recv_sem=recv_sem,
            device_id=where,
            device_id_type=MESH,
        )

    def rs_copy(dest, slot):
        return copy(
            part.at[:, aligned(dest, span)],
            rs_buf.at[slot],
            rs_send.at[dest],
            rs_recv.at[slot],
            {"blk": dest},
        )

    def ag_copy(dest, chunk):
        return copy(
            half_own,
            half.at[:, aligned(chunk, span)],
            ag_send.at[dest],
            ag_recv.at[chunk],
            {"blk": dest},
        )

    def up_copies(c):
        there = {"rows": z + 1}
        return (
            copy(up_out_scale.at[c], up_scale.at[c], us_send.at[c], us_recv.at[c], there),
            copy(up_out.at[c], up_buf.at[c], up_send.at[c], up_recv.at[c], there),
        )

    def down_copies(c):
        there = {"rows": z - 1}
        return (
            copy(down_out_scale.at[c], down_scale.at[c], ds_send.at[c], ds_recv.at[c], there),
            copy(down_out.at[c], down_buf.at[c], down_send.at[c], down_recv.at[c], there),
        )

    def start(copies):
        for each in copies:
            each.start()

    def wait_recv(copies):
        for each in copies:
            each.wait_recv()

    def wait_send(copies):
        for each in copies:
            each.wait_send()

    def gr_copy(dest, slot):
        return copy(
            gram_own, gram_rows.at[slot], gr_send.at[dest], gr_recv.at[slot], {"rows": dest}
        )

    def gb_copy(dest, slot):
        return copy(
            gram_line, gram_blk.at[slot], gb_send.at[dest], gb_recv.at[slot], {"blk": dest}
        )

    piece = width // PIECES
    strip = width // SPLIT

    def bu_copy(c, p):
        k = c * PIECES + p
        chunk = basis.at[:, aligned(k, piece)]
        return copy(chunk, chunk, bu_send.at[k], bu_recv.at[k], {"rows": z + 1})

    def bd_copy(c, p):
        k = c * PIECES + p
        chunk = basis.at[:, aligned(k, piece)]
        return copy(chunk, chunk, bd_send.at[k], bd_recv.at[k], {"rows": z - 1})

    def forward(c):
        return lax.dot_general(
            basis[:, aligned(c, width)],
            dense[:, aligned(c, width)],
            (((1,), (1,)), ((), ())),
            preferred_element_type=F32,
        )

    def backward(k):
        return jnp.dot(half[...], dense[:, aligned(k, strip)], preferred_element_type=F32)

    @pl.loop(0, ITERS)
    def _(it):
        part[...] = forward(z)
        for d in range(1, m):
            for p in range(PIECES):

                @pl.when(jnp.logical_and(it > 0, z - d >= 0))
                def _():
                    bu_copy(z - d, p).wait_recv()

                    @pl.when(z + 1 < m)
                    def _():
                        bu_copy(z - d, p).start()

                @pl.when(jnp.logical_and(it > 0, z + d < m))
                def _():
                    bd_copy(z + d, p).wait_recv()

                    @pl.when(z > 0)
                    def _():
                        bd_copy(z + d, p).start()

            @pl.when(z - d >= 0)
            def _():
                part[...] += forward(z - d)

            @pl.when(z + d < m)
            def _():
                part[...] += forward(z + d)

        @pl.loop(0, owners)
        def _(q):
            @pl.when(q != b)
            def _():
                rs_copy(q, b).start()

        @pl.when(b < owners)
        def _():
            own = part[:, aligned(b, span)]

            def add(d, acc):
                src = lax.rem(b + d, n)
                rs_copy(b, src).wait_recv()
                return acc + rs_buf[src]

            own = lax.fori_loop(1, n, add, own)
            half_own[...] = own.astype(BF16)

            @pl.loop(1, n)
            def _(d):
                ag_copy(lax.rem(b + d, n), b).start()

            half[:, aligned(b, span)] = half_own[...]

        @pl.loop(0, owners)
        def _(q):
            @pl.when(q != b)
            def _():
                ag_copy(b, q).wait_recv()
                rs_copy(q, b).wait_send()

        for k in range(m - 1):
            c = m - 1 - k

            e = k
            for p in range(SPLIT):
                j = c * SPLIT + p

                @pl.when(c > z)
                def _():
                    up_sum[...] = backward(j)

                    @pl.when(z > 0)
                    def _():
                        wait_recv(up_copies(j))
                        up_sum[...] += decode(up_buf.at[j], up_scale.at[j])

                    encode(up_sum[...], up_out.at[j], up_out_scale.at[j])
                    start(up_copies(j))

                i = e * SPLIT + p

                @pl.when(e < z)
                def _():
                    down_sum[...] = backward(i)

                    @pl.when(z < m - 1)
                    def _():
                        wait_recv(down_copies(i))
                        down_sum[...] += decode(down_buf.at[i], down_scale.at[i])

                    encode(down_sum[...], down_out.at[i], down_out_scale.at[i])
                    start(down_copies(i))

        for p in range(SPLIT):
            own = slice(p * strip, (p + 1) * strip)
            j = z * SPLIT + p
            hess_own[:, own] = backward(j)

            @pl.when(z > 0)
            def _():
                wait_recv(up_copies(j))
                hess_own[:, own] += decode(up_buf.at[j], up_scale.at[j])

            @pl.when(z < m - 1)
            def _():
                wait_recv(down_copies(j))
                hess_own[:, own] += decode(down_buf.at[j], down_scale.at[j])

        @pl.when(it > 0)
        def _():
            for c in range(m):
                for p in range(PIECES):

                    @pl.when(jnp.logical_and(c <= z, z + 1 < m))
                    def _():
                        bu_copy(c, p).wait_send()

                    @pl.when(jnp.logical_and(c >= z, z > 0))
                    def _():
                        bd_copy(c, p).wait_send()

        hess = hess_own[...]
        gram = lax.dot_general(
            hess, hess, (((1,), (1,)), ((), ())), precision=HIGHEST, preferred_element_type=F32
        )
        fold = vectors // 2
        gram_own[...] = jnp.concatenate([gram[:fold], gram[fold:]], axis=1)

        @pl.loop(1, m)
        def _(d):
            gr_copy(lax.rem(z + d, m), z).start()

        def add_line(d, acc):
            src = lax.rem(z + d, m)
            gr_copy(z, src).wait_recv()
            return acc + gram_rows[src]

        gram_line[...] = lax.fori_loop(1, m, add_line, gram_own[...])

        @pl.loop(1, n)
        def _(d):
            gb_copy(lax.rem(b + d, n), b).start()

        def add_blk(d, acc):
            src = lax.rem(b + d, n)
            gb_copy(b, src).wait_recv()
            return acc + gram_blk[src]

        packed = lax.fori_loop(1, n, add_blk, gram_line[...])
        gram = jnp.concatenate([packed[:, :vectors], packed[:, vectors:]], axis=0) / total

        for c in range(m):

            @pl.when(c > z)
            def _():
                for p in range(SPLIT):
                    wait_send(up_copies(c * SPLIT + p))

            @pl.when(c < z)
            def _():
                for p in range(SPLIT):
                    wait_send(down_copies(c * SPLIT + p))

        @pl.loop(1, m)
        def _(d):
            gr_copy(lax.rem(z + d, m), z).wait_send()

        @pl.loop(1, n)
        def _(d):
            gb_copy(lax.rem(b + d, n), b).wait_send()

        @pl.when(b < owners)
        def _():
            @pl.loop(1, n)
            def _(d):
                ag_copy(lax.rem(b + d, n), b).wait_send()

        result = jnp.dot(
            inverse_factor(gram), hess_own[...], precision=HIGHEST, preferred_element_type=F32
        )
        basis[:, aligned(z, width)] = result.astype(BF16)

        @pl.when(it < ITERS - 1)
        def _():
            for p in range(PIECES):

                @pl.when(z + 1 < m)
                def _():
                    bu_copy(z, p).start()

                @pl.when(z > 0)
                def _():
                    bd_copy(z, p).start()

        out_ref[it] = result


def local(n, m, sens_tiles, start_basis, row_blocks, col_blocks, live_counts):
    slots, tile = sens_tiles.shape[0], sens_tiles.shape[2]
    vectors, cells = start_basis.shape
    data, width = RB * tile, cells // m
    span = data // min(n, RB)
    numbers = jnp.arange(slots, dtype=jnp.int32)
    places = row_blocks[:, 0] * CB + col_blocks[:, 0]
    hit = (places[None, :] == jnp.arange(RB * CB, dtype=jnp.int32)[:, None]) & (
        numbers < live_counts[0, 0]
    )[None, :]
    inv = jnp.min(jnp.where(hit, numbers[None, :], slots), axis=1)
    total = float(cells * n)
    dma = pltpu.SemaphoreType.DMA
    return pl.pallas_call(
        functools.partial(kernel, n, m, total),
        out_shape=jax.ShapeDtypeStruct((ITERS, vectors, width), F32),
        in_specs=[
            pl.BlockSpec(memory_space=pltpu.SMEM),
            pl.BlockSpec(memory_space=pl.ANY),
            pl.BlockSpec(memory_space=pltpu.VMEM),
        ],
        out_specs=pl.BlockSpec(memory_space=pltpu.VMEM),
        scratch_shapes=[
            pltpu.VMEM((slots + 1, tile, tile), BF16),
            pltpu.VMEM((data, cells), BF16),
            pltpu.VMEM((vectors, cells), BF16),
            pltpu.VMEM((vectors, data), F32),
            pltpu.VMEM((n, vectors, span), F32),
            pltpu.VMEM((vectors, span), BF16),
            pltpu.VMEM((vectors, data), BF16),
            pltpu.VMEM((vectors, width), F32),
            pltpu.VMEM((m * SPLIT, vectors, width // SPLIT), CODE),
            pltpu.VMEM((m * SPLIT, vectors, width // SPLIT), CODE),
            pltpu.VMEM((m * SPLIT, vectors, width // SPLIT), CODE),
            pltpu.VMEM((m * SPLIT, vectors, width // SPLIT), CODE),
            pltpu.VMEM((m * SPLIT, 8, vectors * 2), F32),
            pltpu.VMEM((m * SPLIT, 8, vectors * 2), F32),
            pltpu.VMEM((m * SPLIT, 8, vectors * 2), F32),
            pltpu.VMEM((m * SPLIT, 8, vectors * 2), F32),
            pltpu.VMEM((vectors, width // SPLIT), F32),
            pltpu.VMEM((vectors, width // SPLIT), F32),
            pltpu.VMEM((vectors // 2, vectors * 2), F32),
            pltpu.VMEM((m, vectors // 2, vectors * 2), F32),
            pltpu.VMEM((vectors // 2, vectors * 2), F32),
            pltpu.VMEM((n, vectors // 2, vectors * 2), F32),
            dma,
            dma((n,)),
            dma((n,)),
            dma((n,)),
            dma((n,)),
            dma((m * SPLIT,)),
            dma((m * SPLIT,)),
            dma((m * SPLIT,)),
            dma((m * SPLIT,)),
            dma((m,)),
            dma((m,)),
            dma((n,)),
            dma((n,)),
            dma((m * PIECES,)),
            dma((m * PIECES,)),
            dma((m * PIECES,)),
            dma((m * PIECES,)),
            dma((m * SPLIT,)),
            dma((m * SPLIT,)),
            dma((m * SPLIT,)),
            dma((m * SPLIT,)),
        ],
        compiler_params=pltpu.CompilerParams(
            collective_id=0, has_side_effects=True, vmem_limit_bytes=56 * 1024 * 1024
        ),
        name="subspace",
    )(inv, sens_tiles, start_basis)


def solution(mesh):
    in_specs = (
        P("blk", "rows", None),
        P(None, "blk"),
        P("blk", "rows"),
        P("blk", "rows"),
        P("blk", "rows"),
    )
    out_specs = P(None, None, ("blk", "rows"))
    return jax.shard_map(
        functools.partial(local, mesh.shape["blk"], mesh.shape["rows"]),
        mesh=mesh,
        in_specs=in_specs,
        out_specs=out_specs,
        check_vma=False,
    )
```
